512 devices in a mesh: snap: 32 (over x_hi, y, core), var: 16 (over z, x_lo).
Axes of the slice: x: 4 (x_hi: 2, x_lo: 2; x = x_hi * 2 + x_lo), y: 8, z: 8, core: 2. Of those that a mesh axis runs over, the one named last changes fastest.
Arguments:
- tensor: float32 [512, 1280, 1024], P('var', 'snap'), may hold values from 0.05 to 5
- cell_factor: float32 [1024, 256], P('snap'), may hold values from 0.1 to 1
- var_factor: float32 [512, 256], P('var'), may hold values from 0.1 to 1
- snap_factor: float32 [1280, 256], P('snap'), may hold values from 0.002 to 0.02
Outputs:
- grad_cells: float32 [1024, 256], P('snap')
- grad_vars: float32 [512, 256], P('var')
- grad_snaps: float32 [1280, 256], P('snap')
The draws below stay inside these ranges and needn't reach their ends.
All inputs are finite; a program needn't handle non-finite values.
Results may differ from the reference program's by a relative error of at most 0.0003.
Values sent between devices are 32-bit elements; how exact they have to be, the bound alone decides.
No kernel may reach another device: no remote copies, remote signals or barrier semaphores. Data moves between devices by JAX's collectives and lax.ppermute only.
A program may use at most 64 MiB of HBM per device.

```python
import math
import jax
import jax.numpy as jnp
from jax import lax

V = 512
S = 1280
R = 256
CELLS = 1024
N_VAR = 16


def steps_of(own_key, shape, cuts, smallest, high):
    factor_of, own = 1.0, jax.random.fold_in(own_key, 6)
    for position, blocks in cuts:
        heights = jnp.exp(jax.random.uniform(jax.random.fold_in(own, position), (blocks,), jnp.float32, smallest / len(cuts), high / len(cuts)))
        factor_of = factor_of * jnp.repeat(heights, shape[position] // blocks).reshape([-1 if axis == position else 1 for axis in range(len(shape))])
    return factor_of


def setup_inputs(seed: int = 0) -> dict:
    seeds = jax.random.split(jax.random.key(seed), 5)
    tensor = jnp.clip(jnp.exp(math.log(5.0) - 4.6051702 * jax.random.uniform(seeds[0], (V, S, CELLS), jnp.float32) ** steps_of(seeds[0], (V, S, CELLS), ((0, 16), (1, 32)), -0.2, 0.2)), 0.05, 5.0)
    cell_factor = jnp.clip(0.1 + 0.9 * jax.random.uniform(seeds[1], (CELLS, R), jnp.float32) ** steps_of(seeds[1], (CELLS, R), ((0, 32),), -0.2, 0.2), 0.1, 1.0)
    var_factor = jnp.clip(0.1 + 0.9 * jax.random.uniform(seeds[2], (V, R), jnp.float32) ** steps_of(seeds[2], (V, R), ((0, 16),), -0.2, 0.2), 0.1, 1.0)
    snap_factor = jnp.clip(jnp.exp(math.log(0.02) - 2.30258502 * jax.random.uniform(seeds[3], (S, R), jnp.float32) ** steps_of(seeds[3], (S, R), ((0, 32),), -0.2, 0.2)), 0.002, 0.02)
    return dict(tensor=tensor, cell_factor=cell_factor, var_factor=var_factor, snap_factor=snap_factor)


high = lax.Precision.HIGHEST

def reference(tensor, cell_factor, var_factor, snap_factor):
    block = V // N_VAR
    cells = tensor.shape[2]

    def step(carry, index):
        grad_cell, grad_snap = carry
        start = (index * block).astype(jnp.int32)
        data = lax.dynamic_slice_in_dim(tensor, start, block, 0).reshape(block * S, cells)
        rows_var = lax.dynamic_slice_in_dim(var_factor, start, block, 0)
        khatri = (rows_var[:, None, :] * snap_factor[None, :, :]).reshape(block * S, R)
        model = jnp.dot(khatri, cell_factor.T, precision=high, preferred_element_type=jnp.float32)
        deriv = (model - data) * lax.rsqrt(model)
        grad_cell = grad_cell + jnp.dot(deriv.T, khatri, precision=high, preferred_element_type=jnp.float32)
        folded = jnp.dot(deriv, cell_factor, precision=high, preferred_element_type=jnp.float32).reshape(block, S, R)
        grad_var = jnp.einsum('vsr,sr->vr', folded, snap_factor, precision=high)
        grad_snap = grad_snap + jnp.einsum('vsr,vr->sr', folded, rows_var, precision=high)
        return ((grad_cell, grad_snap), grad_var)
    start_carry = (jnp.zeros((cells, R), jnp.float32), jnp.zeros((S, R), jnp.float32))
    (grad_cells, grad_snaps), pieces = lax.scan(step, start_carry, jnp.arange(N_VAR, dtype=jnp.int32))
    return (grad_cells, pieces.reshape(V, R), grad_snaps)
```

```python
import jax
import jax.numpy as jnp
from jax import lax
from jax.sharding import Mesh, PartitionSpec as P

split3 = lax.Precision.HIGH
exact = lax.Precision.HIGHEST
snaps = ("xh", "y", "core")
rows = ("xh", "y")
variables = ("z", "xl")
swap = [(0, 1), (1, 0)]


def halves(a):
    lead = a.shape[:-2]
    a = a.reshape(*lead, a.shape[-2], 2, 128)
    return jnp.swapaxes(a, -3, -2).reshape(*lead, -1, 128)


def whole(a):
    n = a.shape[0] // 2
    return jnp.swapaxes(a.reshape(2, n, 128), 0, 1).reshape(n, 256)


def exchange(a, axes):
    return lax.all_to_all(a, axes, 0, 0)


def spread(a, axes, n):
    return exchange(jnp.broadcast_to(a[None], (n, *a.shape)), axes)


def local(tensor, cell_factor, var_factor, snap_factor):
    nv, ns, cells = tensor.shape
    own, rank = cell_factor.shape
    groups, peers = cells // own // 2, lax.axis_size(variables)
    core = lax.axis_index("core")
    khatri = (var_factor[:, None, :] * snap_factor[None, :, :]).reshape(nv * ns, rank)
    flat = tensor.reshape(nv * ns, cells)

    mine = spread(cell_factor, rows, groups)
    other = lax.ppermute(mine, "core", swap)
    first, second = jnp.where(core == 0, mine, other), jnp.where(core == 0, other, mine)
    all_cells = jnp.stack([first, second], axis=1).reshape(cells, rank)

    model = jnp.dot(khatri, all_cells.T, precision=split3, preferred_element_type=jnp.float32)
    deriv = (model - flat) * lax.rsqrt(model)
    folded = jnp.dot(deriv, all_cells, precision=split3, preferred_element_type=jnp.float32).reshape(nv, ns, rank)
    part_vars = jnp.einsum("vsr,sr->vr", folded, snap_factor, precision=exact)
    part_snaps = jnp.einsum("vsr,vr->sr", folded, var_factor, precision=exact)
    part_cells = jnp.dot(deriv.T, khatri, precision=split3, preferred_element_type=jnp.float32)
    part_cells = part_cells.reshape(groups, 2, own, rank)

    kept = lax.dynamic_index_in_dim(part_cells, core, 1, keepdims=False)
    given = lax.dynamic_index_in_dim(part_cells, 1 - core, 1, keepdims=False)
    kept = kept + lax.ppermute(given, "core", swap)
    part_vars = part_vars + lax.ppermute(part_vars, "core", swap)

    nc, nw = own * 2, nv * 2 // groups
    sent = jnp.concatenate([halves(kept), halves(part_vars).reshape(groups, nw, 128)], axis=1)
    got = exchange(sent, rows).sum(0)
    cell_sum, var_sum = got[:nc], got[nc:]
    sent = jnp.concatenate(
        [cell_sum.reshape(peers, -1, 128), halves(part_snaps).reshape(peers, -1, 128)], axis=1
    )
    got = exchange(sent, variables).sum(0)
    back = spread(got, variables, peers)
    k = nc // peers
    grad_cells = whole(back[:, :k].reshape(-1, 128))
    grad_snaps = whole(back[:, k:].reshape(-1, 128))
    grad_vars = whole(spread(var_sum, rows, groups).reshape(-1, 128))
    return grad_cells, grad_vars, grad_snaps


def solution(mesh):
    fine = Mesh(mesh.devices.reshape(2, 8, 2, 8, 2), ("xh", "y", "core", "z", "xl"))
    return jax.shard_map(
        local,
        mesh=fine,
        in_specs=(P(variables, snaps, None), P(snaps, None), P(variables, None), P(snaps, None)),
        out_specs=(P(snaps, None), P(variables, None), P(snaps, None)),
        check_vma=False,
    )
```

```python
import jax
import jax.numpy as jnp
from jax import lax
from jax.experimental import pallas as pl
from jax.experimental.pallas import tpu as pltpu
from jax.sharding import Mesh, PartitionSpec as P

snaps = ("xh", "y", "core")
rows = ("xh", "y")
variables = ("z", "xl")
swap = [(0, 1), (1, 0)]
f32, bf16 = jnp.float32, jnp.bfloat16
lanes, frag, tile = 128, 32, 256
vmem = pl.BlockSpec(memory_space=pltpu.VMEM)
hbm = pl.BlockSpec(memory_space=pltpu.HBM)
small = pltpu.CompilerParams(vmem_limit_bytes=8 << 20)


def split(a):
    hi = a.astype(bf16)
    return hi, (a - hi.astype(f32)).astype(bf16)


def dot(a, b):
    return jnp.dot(a, b, preferred_element_type=f32)


def contract(core_ref, tensor_hbm, mine_ref, other_ref, var_hbm, snap_hbm, kept_ref, given_ref, snaps_ref,
             data, var_ref, snap_ref, cells, across, down, total, sems, small_sems):
    groups, own, rank = mine_ref.shape
    blocks, tiles, step, ns, _ = data.shape
    core = core_ref[0]
    loads = [
        [
            pltpu.make_async_copy(
                tensor_hbm.at[pl.ds(b * step, step), :, pl.ds(n * tile, tile)], data.at[b, n], sems.at[b, n]
            )
            for n in range(tiles)
        ]
        for b in range(blocks)
    ]
    factors = [
        pltpu.make_async_copy(snap_hbm, snap_ref, small_sems.at[0]),
        pltpu.make_async_copy(var_hbm, var_ref, small_sems.at[1]),
    ]
    for copy in factors + loads[0] + loads[1]:
        copy.start()
    for g in range(groups):
        cells[pl.ds(pl.multiple_of((2 * g + core) * own, own), own), :] = mine_ref[g]
        cells[pl.ds(pl.multiple_of((2 * g + 1 - core) * own, own), own), :] = other_ref[g]
    for n in range(tiles):
        block = cells[n * tile:(n + 1) * tile, :]
        hi, lo = split(block)
        down[n] = jnp.concatenate([hi, hi, lo], axis=0)
        hi, lo = split(block.T)
        across[n] = jnp.concatenate([hi, hi, lo], axis=0)
    for copy in factors:
        copy.wait()
    snap = snap_ref[...]
    snap_sum = jnp.zeros((ns, rank), f32)
    for b in range(blocks):
        var = var_ref[b * step:(b + 1) * step, :]
        khatri = (var[:, None, :] * snap[None, :, :]).reshape(step * ns, rank)
        hi, lo = split(khatri)
        k3 = jnp.concatenate([hi, lo, hi], axis=1)
        hi, lo = split(khatri.T)
        kt3 = jnp.concatenate([hi, lo, hi], axis=1)
        folded = jnp.zeros((step * ns, rank), f32)
        for n in range(tiles):
            model = dot(k3, across[n])
            loads[b][n].wait()
            hi, lo = split((model - data[b, n].reshape(step * ns, tile)) * lax.rsqrt(model))
            folded = folded + dot(jnp.concatenate([hi, lo, hi], axis=1), down[n])
            part = dot(kt3, jnp.concatenate([hi, hi, lo], axis=0))
            total[n] = part if b == 0 else total[n] + part
        folded = folded.reshape(step, ns, rank)
        sums = (folded * snap[None]).sum(1)
        kept_ref[groups, b * step:(b + 1) * step, :] = sums
        given_ref[groups, b * step:(b + 1) * step, :] = sums
        snap_sum = snap_sum + (folded * var[:, None, :]).sum(0)
    snaps_ref[...] = snap_sum
    for n in range(tiles):
        cells[n * tile:(n + 1) * tile, :] = total[n].T
    for g in range(groups):
        kept_ref[g] = cells[pl.ds(pl.multiple_of((2 * g + core) * own, own), own), :]
        given_ref[g] = cells[pl.ds(pl.multiple_of((2 * g + 1 - core) * own, own), own), :]


def contracted(core, tensor, mine, other, var, snap):
    groups, own, rank = mine.shape
    nv, ns, width = tensor.shape
    blocks, tiles = 2, width // tile
    halfsum = jax.ShapeDtypeStruct((groups + 1, own, rank), f32)
    return pl.pallas_call(
        contract,
        name="contract",
        in_specs=[pl.BlockSpec(memory_space=pltpu.SMEM), hbm, vmem, vmem, hbm, hbm],
        out_specs=[vmem] * 3,
        out_shape=[halfsum, halfsum, jax.ShapeDtypeStruct((ns, rank), f32)],
        scratch_shapes=[
            pltpu.VMEM((blocks, tiles, nv // blocks, ns, tile), f32),
            pltpu.VMEM((nv, rank), f32),
            pltpu.VMEM((ns, rank), f32),
            pltpu.VMEM((width, rank), f32),
            pltpu.VMEM((tiles, 3 * rank, tile), bf16),
            pltpu.VMEM((tiles, 3 * tile, rank), bf16),
            pltpu.VMEM((tiles, rank, tile), f32),
            pltpu.SemaphoreType.DMA((blocks, tiles)),
            pltpu.SemaphoreType.DMA((2,)),
        ],
        compiler_params=pltpu.CompilerParams(vmem_limit_bytes=36 << 20),
        cost_estimate=pl.CostEstimate(
            flops=18 * nv * ns * width * rank, bytes_accessed=4 * nv * ns * width, transcendentals=nv * ns * width
        ),
    )(core.reshape(1), tensor, mine, other, var, snap)


def turn(blocks):
    where = lax.broadcasted_iota(jnp.int32, blocks[0].shape, blocks[0].ndim - 1) // frag

    def pick(choices, at):
        out = choices[at(0)]
        for b in range(1, 4):
            out = jnp.where(where == b, choices[at(b)], out)
        return out

    shifted = []
    for s in range(4):
        y = pick(blocks, lambda b: (b + s) % 4)
        shifted.append(pltpu.roll(y, frag * s, y.ndim - 1) if s else y)
    return [pick(shifted, lambda b: (b - i) % 4) for i in range(4)]


def pack(kept_ref, got_ref, snaps_ref, out_ref):
    own, rank = kept_ref.shape[1:]
    ns = snaps_ref.shape[0]
    zero = jnp.zeros((own, lanes), f32)
    for h in range(rank // lanes):
        side = slice(h * lanes, (h + 1) * lanes)
        for u in range(5):
            if u < 4:
                blocks = [kept_ref[4 * i + u, :, side] + got_ref[4 * i + u, :, side] for i in range(4)]
            else:
                rest = jnp.concatenate([snaps_ref[own:, side], zero[: 2 * own - ns]], axis=0)
                blocks = [kept_ref[16, :, side] + got_ref[16, :, side], snaps_ref[:own, side], rest, zero]
            for i, block in enumerate(turn(blocks)):
                out_ref[pl.ds((4 * h + i) * own * 5 + u, own, stride=5), :] = block


def regroup(got_ref, out_ref):
    n = out_ref.shape[0]
    where = lax.broadcasted_iota(jnp.int32, (1, lanes), 1) // frag
    sums = []
    for u in range(4):
        sums.append(got_ref[pl.ds(u, n, stride=5), :].sum(0, keepdims=True))
    sums = jnp.concatenate(sums, axis=0)
    cells = [pltpu.roll(sums, frag * (3 - i), 1) if i < 3 else sums for i in range(4)]
    rest = got_ref[pl.ds(4, n, stride=5), :].reshape(16, n // 16, lanes)
    var, snap = rest.sum(0), rest.sum(1)
    by_group = jnp.where(where == 3, jnp.concatenate(cells, axis=0), snap)
    out = jnp.where(where[None] == 0, var[None], by_group[:, None, :])
    out_ref[...] = out.reshape(n, lanes)


def unpack(got_ref, cells_ref, var_ref, snap_ref):
    own = cells_ref.shape[0]
    ns = snap_ref.shape[0]
    for h in range(2):
        side = slice(h * lanes, (h + 1) * lanes)
        blocks = [got_ref[(4 * h + i) * own:(4 * h + i + 1) * own, :] for i in range(4)]
        var, first, rest, cells = turn(blocks)
        var_ref[:, side] = var
        snap_ref[:own, side] = first
        snap_ref[own:, side] = rest[: ns - own]
        cells_ref[:, side] = cells


def exchange(a, n):
    out = lax.all_to_all(a.reshape(n, -1, 1, lanes), rows + variables, 0, 0)
    return out.reshape(-1, lanes)


def local(tensor, cell_factor, var_factor, snap_factor):
    groups, peers = lax.axis_size(rows), lax.axis_size(variables)
    n = groups * peers
    mine = lax.all_to_all(jnp.broadcast_to(cell_factor[None], (groups, *cell_factor.shape)), rows, 0, 0)
    other = lax.ppermute(mine, "core", swap)
    kept, given, part_snaps = contracted(
        lax.axis_index("core"), tensor, mine, other, var_factor, snap_factor
    )
    got = lax.ppermute(given, "core", swap)
    sent = pl.pallas_call(
        pack, name="pack", in_specs=[vmem] * 3, out_specs=vmem,
        out_shape=jax.ShapeDtypeStruct((5 * n, lanes), f32), compiler_params=small,
    )(kept, got, part_snaps)
    sent = pl.pallas_call(
        regroup, name="regroup", in_specs=[vmem], out_specs=vmem,
        out_shape=jax.ShapeDtypeStruct((n, lanes), f32), compiler_params=small,
    )(exchange(sent, n))
    return pl.pallas_call(
        unpack, name="unpack", in_specs=[vmem], out_specs=[vmem] * 3,
        out_shape=[jax.ShapeDtypeStruct(a.shape, f32) for a in (cell_factor, var_factor, snap_factor)], compiler_params=small,
    )(exchange(sent, n))


def solution(mesh):
    fine = Mesh(mesh.devices.reshape(2, 8, 2, 8, 2), ("xh", "y", "core", "z", "xl"))
    return jax.shard_map(
        local,
        mesh=fine,
        in_specs=(P(variables, snaps, None), P(snaps, None), P(variables, None), P(snaps, None)),
        out_specs=(P(snaps, None), P(variables, None), P(snaps, None)),
        check_vma=False,
    )
```

```python
import jax
import jax.numpy as jnp
from jax import lax
from jax.experimental import pallas as pl
from jax.experimental.pallas import tpu as pltpu
from jax.sharding import Mesh, PartitionSpec as P

snaps = ("xh", "y", "core")
rows = ("xh", "y")
variables = ("z", "xl")
swap = [(0, 1), (1, 0)]
f32, bf16 = jnp.float32, jnp.bfloat16
lanes, frag, tile = 128, 64, 256
vmem = pl.BlockSpec(memory_space=pltpu.VMEM)
hbm = pl.BlockSpec(memory_space=pltpu.HBM)
small = pltpu.CompilerParams(vmem_limit_bytes=8 << 20)


def hold(a):
    return pltpu.with_memory_space_constraint(a, pltpu.HBM)


def split(a):
    hi = a.astype(bf16)
    return hi, (a - hi.astype(f32)).astype(bf16)


def dot(a, b):
    return jnp.dot(a, b, preferred_element_type=f32)


def contract(core_ref, tensor_hbm, mine_ref, other_ref, var_hbm, snap_hbm, kept_ref, given_ref, snaps_ref,
             data, var_ref, snap_ref, cells, across, down, total, sems, small_sems):
    groups, own, rank = mine_ref.shape
    blocks, tiles, step, ns, _ = data.shape
    core = core_ref[0]
    loads = [
        [
            pltpu.make_async_copy(
                tensor_hbm.at[pl.ds(b * step, step), :, pl.ds(n * tile, tile)], data.at[b, n], sems.at[b, n]
            )
            for n in range(tiles)
        ]
        for b in range(blocks)
    ]
    factors = [
        pltpu.make_async_copy(snap_hbm, snap_ref, small_sems.at[0]),
        pltpu.make_async_copy(var_hbm, var_ref, small_sems.at[1]),
    ]
    for copy in factors + loads[0] + loads[1]:
        copy.start()
    for g in range(groups):
        cells[pl.ds(pl.multiple_of((2 * g + core) * own, own), own), :] = mine_ref[g]
        cells[pl.ds(pl.multiple_of((2 * g + 1 - core) * own, own), own), :] = other_ref[g]
    for n in range(tiles):
        block = cells[n * tile:(n + 1) * tile, :]
        hi, lo = split(block)
        down[n] = jnp.concatenate([hi, hi, lo], axis=0)
        hi, lo = split(block.T)
        across[n] = jnp.concatenate([hi, hi, lo], axis=0)
    for copy in factors:
        copy.wait()
    snap = snap_ref[...]
    snap_sum = jnp.zeros((ns, rank), f32)
    for b in range(blocks):
        var = var_ref[b * step:(b + 1) * step, :]
        khatri = (var[:, None, :] * snap[None, :, :]).reshape(step * ns, rank)
        hi, lo = split(khatri)
        k3 = jnp.concatenate([hi, lo, hi], axis=1)
        hi, lo = split(khatri.T)
        kt3 = jnp.concatenate([hi, lo, hi], axis=1)
        folded = jnp.zeros((step * ns, rank), f32)
        for n in range(tiles):
            model = dot(k3, across[n])
            loads[b][n].wait()
            hi, lo = split((model - data[b, n].reshape(step * ns, tile)) * lax.rsqrt(model))
            folded = folded + dot(jnp.concatenate([hi, lo, hi], axis=1), down[n])
            part = dot(kt3, jnp.concatenate([hi, hi, lo], axis=0))
            total[n] = part if b == 0 else total[n] + part
        folded = folded.reshape(step, ns, rank)
        sums = (folded * snap[None]).sum(1)
        kept_ref[groups, b * step:(b + 1) * step, :] = sums
        given_ref[groups, b * step:(b + 1) * step, :] = sums
        snap_sum = snap_sum + (folded * var[:, None, :]).sum(0)
    snaps_ref[...] = snap_sum
    for n in range(tiles):
        cells[n * tile:(n + 1) * tile, :] = total[n].T
    for g in range(groups):
        kept_ref[g] = cells[pl.ds(pl.multiple_of((2 * g + core) * own, own), own), :]
        given_ref[g] = cells[pl.ds(pl.multiple_of((2 * g + 1 - core) * own, own), own), :]


def contracted(core, tensor, mine, other, var, snap):
    groups, own, rank = mine.shape
    nv, ns, width = tensor.shape
    blocks, tiles = 2, width // tile
    halfsum = jax.ShapeDtypeStruct((groups + 1, own, rank), f32)
    return pl.pallas_call(
        contract,
        name="contract",
        in_specs=[pl.BlockSpec(memory_space=pltpu.SMEM), hbm, vmem, vmem, hbm, hbm],
        out_specs=[vmem] * 3,
        out_shape=[halfsum, halfsum, jax.ShapeDtypeStruct((ns, rank), f32)],
        scratch_shapes=[
            pltpu.VMEM((blocks, tiles, nv // blocks, ns, tile), f32),
            pltpu.VMEM((nv, rank), f32),
            pltpu.VMEM((ns, rank), f32),
            pltpu.VMEM((width, rank), f32),
            pltpu.VMEM((tiles, 3 * rank, tile), bf16),
            pltpu.VMEM((tiles, 3 * tile, rank), bf16),
            pltpu.VMEM((tiles, rank, tile), f32),
            pltpu.SemaphoreType.DMA((blocks, tiles)),
            pltpu.SemaphoreType.DMA((2,)),
        ],
        compiler_params=pltpu.CompilerParams(vmem_limit_bytes=36 << 20),
        cost_estimate=pl.CostEstimate(
            flops=18 * nv * ns * width * rank, bytes_accessed=4 * nv * ns * width, transcendentals=nv * ns * width
        ),
    )(core, hold(tensor), mine, other, hold(var), hold(snap))


def turn(a, b):
    low = lax.broadcasted_iota(jnp.int32, a.shape, a.ndim - 1) < frag
    axis = a.ndim - 1
    return jnp.where(low, a, pltpu.roll(b, frag, axis)), jnp.where(low, pltpu.roll(a, frag, axis), b)


def pack(kept_ref, got_ref, snaps_ref, out_ref):
    own, rank = kept_ref.shape[1:]
    ns = snaps_ref.shape[0]
    n = out_ref.shape[0] // 6
    zero = jnp.zeros((own, lanes), f32)

    def put(x, h, u, a, b):
        for i, block in enumerate(turn(a, b)):
            out_ref[pl.ds((x * n // 2 + (2 * h + i) * own) * 6 + u, own, stride=6), :] = block

    for h in range(rank // lanes):
        side = slice(h * lanes, (h + 1) * lanes)
        total = lambda g: kept_ref[g, :, side] + got_ref[g, :, side]
        rest = jnp.concatenate([snaps_ref[own:, side], zero[: 2 * own - ns]], axis=0)
        for x in range(2):
            for u in range(4):
                put(x, h, u, total(8 * x + u), total(8 * x + 4 + u))
            put(x, h, 4, total(16), snaps_ref[:own, side])
            put(x, h, 5, rest, zero)


def regroup(x_ref, got_ref, out_ref):
    n = got_ref.shape[0] // 6
    low = lax.broadcasted_iota(jnp.int32, (1, lanes), 1) < frag
    first = x_ref[1] == 0
    unit = lambda u: got_ref[pl.ds(u, n, stride=6), :]
    sums = jnp.concatenate([unit(u).sum(0, keepdims=True) for u in range(4)], axis=0)
    cells = jnp.concatenate([pltpu.roll(sums, frag, 1), sums], axis=0)
    mixed = unit(4).reshape(16, n // 16, lanes)
    var, head = mixed.sum(0), mixed.sum(1)
    rest = unit(5).reshape(16, n // 16, lanes).sum(1)
    snap = jnp.where(low, rest, head)
    snap = jnp.where(first, snap[:8], snap[8:])
    shape = (8, n // 16, lanes)
    out = jnp.where(low[None], var[None], cells[:, None, :])
    out_ref[pl.ds(0, n // 2, stride=2), :] = out.reshape(n // 2, lanes)
    out_ref[pl.ds(1, n // 2, stride=2), :] = jnp.broadcast_to(snap[:, None, :], shape).reshape(n // 2, lanes)


def unpack(got_ref, cells_ref, var_ref, snap_ref):
    own = cells_ref.shape[0]
    ns = snap_ref.shape[0]
    for h in range(2):
        side = slice(h * lanes, (h + 1) * lanes)
        part = lambda i, u: got_ref[pl.ds(2 * (2 * h + i) * own + u, own, stride=2), :]
        var, cells = turn(part(0, 0), part(1, 0))
        rest, first = turn(part(0, 1), part(1, 1))
        var_ref[:, side] = var
        snap_ref[:own, side] = first
        snap_ref[own:, side] = rest[: ns - own]
        cells_ref[:, side] = cells


def exchange(a, n, axes):
    return lax.all_to_all(a.reshape(n, -1, 1, lanes), axes, 0, 0).reshape(-1, lanes)


def local(tensor, cell_factor, var_factor, snap_factor):
    groups, peers = lax.axis_size(rows), lax.axis_size(variables)
    n = groups * peers
    mine = lax.all_to_all(jnp.broadcast_to(cell_factor[None], (groups, *cell_factor.shape)), rows, 0, 0)
    other = lax.ppermute(mine, "core", swap)
    where = jnp.stack([lax.axis_index("core"), lax.axis_index("xh")])
    kept, given, part_snaps = contracted(
        where, tensor, mine, other, var_factor, snap_factor
    )
    got = lax.ppermute(given, "core", swap)
    sent = pl.pallas_call(
        pack, name="pack", in_specs=[vmem] * 3, out_specs=vmem,
        out_shape=jax.ShapeDtypeStruct((6 * n, lanes), f32), compiler_params=small,
    )(kept, got, part_snaps)
    sent = pl.pallas_call(
        regroup, name="regroup", in_specs=[pl.BlockSpec(memory_space=pltpu.SMEM), vmem], out_specs=vmem,
        out_shape=jax.ShapeDtypeStruct((n, lanes), f32), compiler_params=small,
    )(where, exchange(sent, n, rows + variables))
    return pl.pallas_call(
        unpack, name="unpack", in_specs=[vmem], out_specs=[vmem] * 3,
        out_shape=[jax.ShapeDtypeStruct(a.shape, f32) for a in (cell_factor, var_factor, snap_factor)], compiler_params=small,
    )(exchange(sent, n // 2, ("y",) + variables))


def solution(mesh):
    fine = Mesh(mesh.devices.reshape(2, 8, 2, 8, 2), ("xh", "y", "core", "z", "xl"))
    return jax.shard_map(
        local,
        mesh=fine,
        in_specs=(P(variables, snaps, None), P(snaps, None), P(variables, None), P(snaps, None)),
        out_specs=(P(snaps, None), P(variables, None), P(snaps, None)),
        check_vma=False,
    )
```

```python
import jax
import jax.numpy as jnp
from jax import lax
from jax.experimental import pallas as pl
from jax.experimental.pallas import tpu as pltpu
from jax.sharding import Mesh, PartitionSpec as P

snaps = ("xh", "y", "core")
rows = ("xh", "y")
variables = ("z", "xl")
swap = [(0, 1), (1, 0)]
f32, bf16 = jnp.float32, jnp.bfloat16
lanes, frag, tile = 128, 64, 256
vmem = pl.BlockSpec(memory_space=pltpu.VMEM)
hbm = pl.BlockSpec(memory_space=pltpu.HBM)
small = pltpu.CompilerParams(vmem_limit_bytes=8 << 20)


def hold(a):
    return pltpu.with_memory_space_constraint(a, pltpu.HBM)


def split(a):
    hi = a.astype(bf16)
    return hi, (a - hi.astype(f32)).astype(bf16)


def dot(a, b):
    return jnp.dot(a, b, preferred_element_type=f32)


def prepare(tensor_hbm, var_hbm, snap_hbm, data_ref, khatri_ref, flipped_ref, var_ref, snap_ref, sems, small_sems):
    blocks, n_rows, rank = khatri_ref.shape[0], khatri_ref.shape[1], khatri_ref.shape[2] // 2
    step = data_ref.shape[0] // blocks
    factors = [
        pltpu.make_async_copy(snap_hbm, snap_ref, small_sems.at[0]),
        pltpu.make_async_copy(var_hbm, var_ref, small_sems.at[1]),
    ]
    loads = [
        pltpu.make_async_copy(tensor_hbm.at[pl.ds(b * step, step)], data_ref.at[pl.ds(b * step, step)], sems.at[b])
        for b in range(blocks)
    ]
    for copy in factors + loads:
        copy.start()
    for copy in factors:
        copy.wait()
    for b in range(blocks):
        khatri = var_ref[b * step:(b + 1) * step, :][:, None, :] * snap_ref[...][None, :, :]
        khatri = khatri.reshape(n_rows, rank)
        hi, lo = split(khatri)
        khatri_ref[b, :, :rank] = hi
        khatri_ref[b, :, rank:] = lo
        hi, lo = split(khatri.T)
        flipped_ref[b, :, :n_rows] = hi
        flipped_ref[b, :, n_rows:] = lo
    for copy in loads:
        copy.wait()


def prepared(tensor, var, snap):
    nv, ns, width = tensor.shape
    rank = var.shape[1]
    blocks = 2
    return pl.pallas_call(
        prepare,
        name="prepare",
        in_specs=[hbm] * 3,
        out_specs=[vmem] * 5,
        out_shape=[
            jax.ShapeDtypeStruct(tensor.shape, f32),
            jax.ShapeDtypeStruct((blocks, nv * ns // blocks, 2 * rank), bf16),
            jax.ShapeDtypeStruct((blocks, rank, 2 * nv * ns // blocks), bf16),
            jax.ShapeDtypeStruct(var.shape, f32),
            jax.ShapeDtypeStruct(snap.shape, f32),
        ],
        scratch_shapes=[pltpu.SemaphoreType.DMA((blocks,)), pltpu.SemaphoreType.DMA((2,))],
        compiler_params=small,
        cost_estimate=pl.CostEstimate(flops=0, bytes_accessed=8 * nv * ns * width, transcendentals=0),
    )(hold(tensor), hold(var), hold(snap))


def contract(where_ref, data_ref, khatri_ref, flipped_ref, var_ref, snap_ref, mine_ref, other_ref,
             kept_ref, given_ref, snaps_ref, across, down, total):
    groups, own, rank = mine_ref.shape
    nv, ns, width = data_ref.shape
    blocks, n_rows = khatri_ref.shape[:2]
    tiles, step, per = width // tile, nv // blocks, tile // own // 2
    even = where_ref[0] == 0

    def sides(a, b):
        return jnp.where(even, a, b), jnp.where(even, b, a)

    snap_sum = jnp.zeros((ns, rank), f32)
    for b in range(blocks):
        k2, kt2 = khatri_ref[b], flipped_ref[b]
        k3 = jnp.concatenate([k2, k2[:, :rank]], axis=1)
        kt3 = jnp.concatenate([kt2, kt2[:, :n_rows]], axis=1)
        folded = jnp.zeros((n_rows, rank), f32)
        for n in range(tiles):
            if b == 0:
                block = [part for g in range(n * per, (n + 1) * per) for part in sides(mine_ref[g], other_ref[g])]
                block = jnp.concatenate(block, axis=0)
                hi, lo = split(block)
                down[n] = jnp.concatenate([hi, hi, lo], axis=0)
                hi, lo = split(block.T)
                across[n] = jnp.concatenate([hi, hi, lo], axis=0)
            model = dot(k3, across[n])
            data = data_ref[b * step:(b + 1) * step, :, n * tile:(n + 1) * tile].reshape(n_rows, tile)
            hi, lo = split((model - data) * lax.rsqrt(model))
            folded = folded + dot(jnp.concatenate([hi, lo, hi], axis=1), down[n])
            part = dot(kt3, jnp.concatenate([hi, hi, lo], axis=0))
            if b == 0:
                total[n] = part
            else:
                block = (total[n] + part).T
                for i in range(per):
                    first, second = block[2 * i * own:(2 * i + 1) * own], block[(2 * i + 1) * own:(2 * i + 2) * own]
                    kept_ref[n * per + i], given_ref[n * per + i] = sides(first, second)
        folded = folded.reshape(step, ns, rank)
        sums = (folded * snap_ref[...][None]).sum(1)
        kept_ref[groups, b * step:(b + 1) * step, :] = sums
        given_ref[groups, b * step:(b + 1) * step, :] = sums
        snap_sum = snap_sum + (folded * var_ref[b * step:(b + 1) * step, :][:, None, :]).sum(0)
    snaps_ref[...] = snap_sum


def contracted(where, ready, mine, other):
    groups, own, rank = mine.shape
    nv, ns, width = ready[0].shape
    tiles = width // tile
    halfsum = jax.ShapeDtypeStruct((groups + 1, own, rank), f32)
    return pl.pallas_call(
        contract,
        name="contract",
        in_specs=[pl.BlockSpec(memory_space=pltpu.SMEM)] + [vmem] * 7,
        out_specs=[vmem] * 3,
        out_shape=[halfsum, halfsum, jax.ShapeDtypeStruct((ns, rank), f32)],
        scratch_shapes=[
            pltpu.VMEM((tiles, 3 * rank, tile), bf16),
            pltpu.VMEM((tiles, 3 * tile, rank), bf16),
            pltpu.VMEM((tiles, rank, tile), f32),
        ],
        compiler_params=pltpu.CompilerParams(vmem_limit_bytes=24 << 20),
        cost_estimate=pl.CostEstimate(
            flops=18 * nv * ns * width * rank, bytes_accessed=4 * nv * ns * width, transcendentals=nv * ns * width
        ),
    )(where, *ready, mine, other)


def turn(a, b):
    low = lax.broadcasted_iota(jnp.int32, a.shape, a.ndim - 1) < frag
    axis = a.ndim - 1
    return jnp.where(low, a, pltpu.roll(b, frag, axis)), jnp.where(low, pltpu.roll(a, frag, axis), b)


def pack(kept_ref, got_ref, snaps_ref, out_ref):
    own, rank = kept_ref.shape[1:]
    ns = snaps_ref.shape[0]
    n = out_ref.shape[0] // 6
    zero = jnp.zeros((own, lanes), f32)

    def put(x, h, u, a, b):
        for i, block in enumerate(turn(a, b)):
            out_ref[pl.ds((x * n // 2 + (2 * h + i) * own) * 6 + u, own, stride=6), :] = block

    for h in range(rank // lanes):
        side = slice(h * lanes, (h + 1) * lanes)
        total = lambda g: kept_ref[g, :, side] + got_ref[g, :, side]
        rest = jnp.concatenate([snaps_ref[own:, side], zero[: 2 * own - ns]], axis=0)
        for x in range(2):
            for u in range(4):
                put(x, h, u, total(8 * x + u), total(8 * x + 4 + u))
            put(x, h, 4, total(16), snaps_ref[:own, side])
            put(x, h, 5, rest, zero)


def regroup(x_ref, got_ref, out_ref):
    n = got_ref.shape[0] // 6
    low = lax.broadcasted_iota(jnp.int32, (1, lanes), 1) < frag
    first = x_ref[1] == 0
    unit = lambda u: got_ref[pl.ds(u, n, stride=6), :]
    sums = got_ref[...].reshape(n // 4, 24, lanes).sum(0).reshape(4, 6, lanes).sum(0)[:4]
    cells = jnp.concatenate([pltpu.roll(sums, frag, 1), sums], axis=0)
    mixed = unit(4).reshape(16, n // 16, lanes)
    var, head = mixed.sum(0), mixed.sum(1)
    rest = unit(5).reshape(16, n // 16, lanes).sum(1)
    snap = jnp.where(low, rest, head)
    snap = jnp.where(first, snap[:8], snap[8:])
    shape = (8, n // 16, lanes)
    out = jnp.where(low[None], var[None], cells[:, None, :])
    out_ref[pl.ds(0, n // 2, stride=2), :] = out.reshape(n // 2, lanes)
    out_ref[pl.ds(1, n // 2, stride=2), :] = jnp.broadcast_to(snap[:, None, :], shape).reshape(n // 2, lanes)


def unpack(got_ref, cells_ref, var_ref, snap_ref):
    own = cells_ref.shape[0]
    ns = snap_ref.shape[0]
    for h in range(2):
        side = slice(h * lanes, (h + 1) * lanes)
        part = lambda i, u: got_ref[pl.ds(2 * (2 * h + i) * own + u, own, stride=2), :]
        var, cells = turn(part(0, 0), part(1, 0))
        rest, first = turn(part(0, 1), part(1, 1))
        var_ref[:, side] = var
        snap_ref[:own, side] = first
        snap_ref[own:, side] = rest[: ns - own]
        cells_ref[:, side] = cells


def exchange(a, n, axes):
    return lax.all_to_all(a.reshape(n, -1, 1, lanes), axes, 0, 0).reshape(-1, lanes)


def local(tensor, cell_factor, var_factor, snap_factor):
    groups, peers = lax.axis_size(rows), lax.axis_size(variables)
    n = groups * peers
    mine = lax.all_to_all(jnp.broadcast_to(cell_factor[None], (groups, *cell_factor.shape)), rows, 0, 0)
    other = lax.ppermute(mine, "core", swap)
    where = jnp.stack([lax.axis_index("core"), lax.axis_index("xh")])
    ready = prepared(tensor, var_factor, snap_factor)
    kept, given, part_snaps = contracted(where, ready, mine, other)
    got = lax.ppermute(given, "core", swap)
    sent = pl.pallas_call(
        pack, name="pack", in_specs=[vmem] * 3, out_specs=vmem,
        out_shape=jax.ShapeDtypeStruct((6 * n, lanes), f32), compiler_params=small,
    )(kept, got, part_snaps)
    sent = pl.pallas_call(
        regroup, name="regroup", in_specs=[pl.BlockSpec(memory_space=pltpu.SMEM), vmem], out_specs=vmem,
        out_shape=jax.ShapeDtypeStruct((n, lanes), f32), compiler_params=small,
    )(where, exchange(sent, n, rows + variables))
    return pl.pallas_call(
        unpack, name="unpack", in_specs=[vmem], out_specs=[vmem] * 3,
        out_shape=[jax.ShapeDtypeStruct(a.shape, f32) for a in (cell_factor, var_factor, snap_factor)], compiler_params=small,
    )(exchange(sent, n // 2, ("y",) + variables))


def solution(mesh):
    fine = Mesh(mesh.devices.reshape(2, 8, 2, 8, 2), ("xh", "y", "core", "z", "xl"))
    return jax.shard_map(
        local,
        mesh=fine,
        in_specs=(P(variables, snaps, None), P(snaps, None), P(variables, None), P(snaps, None)),
        out_specs=(P(snaps, None), P(variables, None), P(snaps, None)),
        check_vma=False,
    )
```

```python
import jax
import jax.numpy as jnp
from jax import lax
from jax.experimental import pallas as pl
from jax.experimental.pallas import tpu as pltpu
from jax.sharding import Mesh, PartitionSpec as P

snaps = ("xh", "y", "core")
rows = ("xh", "y")
variables = ("z", "xl")
swap = [(0, 1), (1, 0)]
f32, bf16 = jnp.float32, jnp.bfloat16
lanes, tile = 128, 256
vmem = pl.BlockSpec(memory_space=pltpu.VMEM)
hbm = pl.BlockSpec(memory_space=pltpu.HBM)
small = pltpu.CompilerParams(vmem_limit_bytes=8 << 20)


def hold(a):
    return pltpu.with_memory_space_constraint(a, pltpu.HBM)


def split(a):
    hi = a.astype(bf16)
    return hi, (a - hi.astype(f32)).astype(bf16)


def dot(a, b):
    return jnp.dot(a, b, preferred_element_type=f32)


def prepare(tensor_hbm, var_hbm, snap_hbm, data_ref, khatri_ref, flipped_ref, var_ref, snap_ref, sems, small_sems):
    blocks, n_rows, rank = khatri_ref.shape[0], khatri_ref.shape[1], khatri_ref.shape[2] // 2
    step = data_ref.shape[0] // blocks
    factors = [
        pltpu.make_async_copy(snap_hbm, snap_ref, small_sems.at[0]),
        pltpu.make_async_copy(var_hbm, var_ref, small_sems.at[1]),
    ]
    loads = [
        pltpu.make_async_copy(tensor_hbm.at[pl.ds(b * step, step)], data_ref.at[pl.ds(b * step, step)], sems.at[b])
        for b in range(blocks)
    ]
    for copy in factors + loads:
        copy.start()
    for copy in factors:
        copy.wait()
    for b in range(blocks):
        khatri = var_ref[b * step:(b + 1) * step, :][:, None, :] * snap_ref[...][None, :, :]
        khatri = khatri.reshape(n_rows, rank)
        hi, lo = split(khatri)
        khatri_ref[b, :, :rank] = hi
        khatri_ref[b, :, rank:] = lo
        hi, lo = split(khatri.T)
        flipped_ref[b, :, :n_rows] = hi
        flipped_ref[b, :, n_rows:] = lo
    for copy in loads:
        copy.wait()


def prepared(tensor, var, snap):
    nv, ns, width = tensor.shape
    rank = var.shape[1]
    blocks = 2
    return pl.pallas_call(
        prepare,
        name="prepare",
        in_specs=[hbm] * 3,
        out_specs=[vmem] * 5,
        out_shape=[
            jax.ShapeDtypeStruct(tensor.shape, f32),
            jax.ShapeDtypeStruct((blocks, nv * ns // blocks, 2 * rank), bf16),
            jax.ShapeDtypeStruct((blocks, rank, 2 * nv * ns // blocks), bf16),
            jax.ShapeDtypeStruct(var.shape, f32),
            jax.ShapeDtypeStruct(snap.shape, f32),
        ],
        scratch_shapes=[pltpu.SemaphoreType.DMA((blocks,)), pltpu.SemaphoreType.DMA((2,))],
        compiler_params=small,
        cost_estimate=pl.CostEstimate(flops=0, bytes_accessed=8 * nv * ns * width, transcendentals=0),
    )(hold(tensor), hold(var), hold(snap))


def contract(where_ref, data_ref, khatri_ref, flipped_ref, var_ref, snap_ref, mine_ref, other_ref,
             kept_ref, given_ref, snaps_ref, across, down, total):
    groups, own, rank = mine_ref.shape
    nv, ns, width = data_ref.shape
    blocks, n_rows = khatri_ref.shape[:2]
    tiles, step, per = width // tile, nv // blocks, tile // own // 2
    even = where_ref[0] == 0

    def sides(a, b):
        return jnp.where(even, a, b), jnp.where(even, b, a)

    snap_sum = jnp.zeros((ns, rank), f32)
    for b in range(blocks):
        k2, kt2 = khatri_ref[b], flipped_ref[b]
        k3 = jnp.concatenate([k2, k2[:, :rank]], axis=1)
        kt3 = jnp.concatenate([kt2, kt2[:, :n_rows]], axis=1)
        folded = jnp.zeros((n_rows, rank), f32)
        for n in range(tiles):
            if b == 0:
                block = [part for g in range(n * per, (n + 1) * per) for part in sides(mine_ref[g], other_ref[g])]
                block = jnp.concatenate(block, axis=0)
                hi, lo = split(block)
                down[n] = jnp.concatenate([hi, hi, lo], axis=0)
                hi, lo = split(block.T)
                across[n] = jnp.concatenate([hi, hi, lo], axis=0)
            model = dot(k3, across[n])
            data = data_ref[b * step:(b + 1) * step, :, n * tile:(n + 1) * tile].reshape(n_rows, tile)
            hi, lo = split((model - data) * lax.rsqrt(model))
            folded = folded + dot(jnp.concatenate([hi, lo, hi], axis=1), down[n])
            part = dot(kt3, jnp.concatenate([hi, hi, lo], axis=0))
            if b == 0:
                total[n] = part
            else:
                block = (total[n] + part).T
                for i in range(per):
                    first, second = block[2 * i * own:(2 * i + 1) * own], block[(2 * i + 1) * own:(2 * i + 2) * own]
                    kept_ref[n * per + i], given_ref[n * per + i] = sides(first, second)
        folded = folded.reshape(step, ns, rank)
        sums = (folded * snap_ref[...][None]).sum(1)
        kept_ref[groups, b * step:(b + 1) * step, :] = sums
        given_ref[groups, b * step:(b + 1) * step, :] = sums
        snap_sum = snap_sum + (folded * var_ref[b * step:(b + 1) * step, :][:, None, :]).sum(0)
    snaps_ref[...] = snap_sum


def contracted(where, ready, mine, other):
    groups, own, rank = mine.shape
    nv, ns, width = ready[0].shape
    tiles = width // tile
    halfsum = jax.ShapeDtypeStruct((groups + 1, own, rank), f32)
    return pl.pallas_call(
        contract,
        name="contract",
        in_specs=[pl.BlockSpec(memory_space=pltpu.SMEM)] + [vmem] * 7,
        out_specs=[vmem] * 3,
        out_shape=[halfsum, halfsum, jax.ShapeDtypeStruct((ns, rank), f32)],
        scratch_shapes=[
            pltpu.VMEM((tiles, 3 * rank, tile), bf16),
            pltpu.VMEM((tiles, 3 * tile, rank), bf16),
            pltpu.VMEM((tiles, rank, tile), f32),
        ],
        compiler_params=pltpu.CompilerParams(vmem_limit_bytes=24 << 20),
        cost_estimate=pl.CostEstimate(
            flops=18 * nv * ns * width * rank, bytes_accessed=4 * nv * ns * width, transcendentals=nv * ns * width
        ),
    )(where, *ready, mine, other)


units = 19


def pack(kept_ref, got_ref, snaps_ref, out_ref):
    own, rank = kept_ref.shape[1:]
    ns = snaps_ref.shape[0]
    for h in range(rank // lanes):
        side = slice(h * lanes, (h + 1) * lanes)
        rest = jnp.concatenate([snaps_ref[own:, side], jnp.zeros((2 * own - ns, lanes), f32)], axis=0)
        for u in range(units):
            if u < 17:
                block = kept_ref[u, :, side] + got_ref[u, :, side]
            else:
                block = snaps_ref[:own, side] if u == 17 else rest
            out_ref[pl.ds(h * own * units + u, own, stride=units), :] = block


def regroup(got_ref, out_ref):
    n = got_ref.shape[0] // units
    unit = lambda u: got_ref[pl.ds(u, n, stride=units), :]
    cells = jnp.concatenate([unit(u).sum(0, keepdims=True) for u in range(16)], axis=0)
    grid = lambda u: unit(u).reshape(8, 8, lanes)
    rest = jnp.concatenate([grid(16).sum(0), grid(17).sum(1), grid(18).sum(1)], axis=0)
    for x in range(4):
        out_ref[x, :8, :] = cells[8 * (x // 2):8 * (x // 2) + 8]
        out_ref[x, 8:, :] = rest


def combine(where_ref, got_ref, out_ref):
    n = out_ref.shape[0] // 4
    high, low = where_ref[1] == 0, where_ref[2] == 0
    part = lambda x, i, k: got_ref[x, 8 * i:8 * (i + k), :]
    cells = part(0, 0, 1) + part(1, 0, 1) + part(2, 0, 1) + part(3, 0, 1)
    var = jnp.where(low, part(0, 1, 1) + part(2, 1, 1), part(1, 1, 1) + part(3, 1, 1))
    snap = jnp.where(high, part(0, 2, 2) + part(1, 2, 2), part(2, 2, 2) + part(3, 2, 2))
    shape = (8, 8, lanes)
    for u, rows_of in enumerate([cells[:, None], var[None], snap[:8][:, None], snap[8:][:, None]]):
        out_ref[pl.ds(u, n, stride=4), :] = jnp.broadcast_to(rows_of, shape).reshape(n, lanes)


def unpack(got_ref, cells_ref, var_ref, snap_ref):
    own = cells_ref.shape[0]
    ns = snap_ref.shape[0]
    for h in range(2):
        side = slice(h * lanes, (h + 1) * lanes)
        part = lambda u, k: got_ref[pl.ds(4 * h * own + u, k, stride=4), :]
        cells_ref[:, side] = part(0, own)
        var_ref[:, side] = part(1, own)
        snap_ref[:own, side] = part(2, own)
        snap_ref[own:, side] = part(3, ns - own)


plane = ("y", "z")


def exchange(a, n, axes):
    return lax.all_to_all(a.reshape(n, -1, 1, lanes), axes, 0, 0).reshape(-1, lanes)


def local(tensor, cell_factor, var_factor, snap_factor):
    groups, n = lax.axis_size(rows), lax.axis_size(plane)
    mine = lax.all_to_all(jnp.broadcast_to(cell_factor[None], (groups, *cell_factor.shape)), rows, 0, 0)
    other = lax.ppermute(mine, "core", swap)
    where = jnp.stack([lax.axis_index("core"), lax.axis_index("xh"), lax.axis_index("xl")])
    ready = prepared(tensor, var_factor, snap_factor)
    kept, given, part_snaps = contracted(where, ready, mine, other)
    got = lax.ppermute(given, "core", swap)

    def call(kernel, shapes, *args):
        scalars = sum(a.dtype == jnp.int32 for a in args)
        return pl.pallas_call(
            kernel,
            name=kernel.__name__,
            in_specs=[pl.BlockSpec(memory_space=pltpu.SMEM)] * scalars + [vmem] * (len(args) - scalars),
            out_specs=[vmem] * len(shapes),
            out_shape=[jax.ShapeDtypeStruct(shape, f32) for shape in shapes],
            compiler_params=small,
        )(*args)

    (sent,) = call(pack, [(units * n, lanes)], kept, got, part_snaps)
    (sent,) = call(regroup, [(4, 32, lanes)], exchange(sent, n, plane))
    sent = lax.all_to_all(sent, ("xh", "xl"), 0, 0)
    (sent,) = call(combine, [(4 * n, lanes)], where, sent)
    return tuple(
        call(unpack, [a.shape for a in (cell_factor, var_factor, snap_factor)], exchange(sent, n, plane))
    )


def solution(mesh):
    fine = Mesh(mesh.devices.reshape(2, 8, 2, 8, 2), ("xh", "y", "core", "z", "xl"))
    return jax.shard_map(
        local,
        mesh=fine,
        in_specs=(P(variables, snaps, None), P(snaps, None), P(variables, None), P(snaps, None)),
        out_specs=(P(snaps, None), P(variables, None), P(snaps, None)),
        check_vma=False,
    )
```

```python
import jax
import jax.numpy as jnp
from jax import lax
from jax.experimental import pallas as pl
from jax.experimental.pallas import tpu as pltpu
from jax.sharding import Mesh, PartitionSpec as P

snaps = ("xh", "y", "core")
rows = ("xh", "y")
variables = ("z", "xl")
swap = [(0, 1), (1, 0)]
f32, bf16 = jnp.float32, jnp.bfloat16
lanes, tile = 128, 256
vmem = pl.BlockSpec(memory_space=pltpu.VMEM)
hbm = pl.BlockSpec(memory_space=pltpu.HBM)
small = pltpu.CompilerParams(vmem_limit_bytes=8 << 20)


def hold(a):
    return pltpu.with_memory_space_constraint(a, pltpu.HBM)


def split(a):
    hi = a.astype(bf16)
    return hi, (a - hi.astype(f32)).astype(bf16)


def dot(a, b):
    return jnp.dot(a, b, preferred_element_type=f32)


def prepare(tensor_hbm, var_hbm, snap_hbm, data_ref, khatri_ref, flipped_ref, var_ref, snap_ref, sem, small_sems):
    blocks, n_rows, rank = khatri_ref.shape[0], khatri_ref.shape[1], khatri_ref.shape[2] // 2
    step = data_ref.shape[0]
    factors = [
        pltpu.make_async_copy(snap_hbm, snap_ref, small_sems.at[0]),
        pltpu.make_async_copy(var_hbm, var_ref, small_sems.at[1]),
    ]
    loads = [pltpu.make_async_copy(tensor_hbm.at[pl.ds(0, step)], data_ref, sem)]
    for copy in factors + loads:
        copy.start()
    for copy in factors:
        copy.wait()
    for b in range(blocks):
        khatri = var_ref[b * step:(b + 1) * step, :][:, None, :] * snap_ref[...][None, :, :]
        khatri = khatri.reshape(n_rows, rank)
        hi, lo = split(khatri)
        khatri_ref[b, :, :rank] = hi
        khatri_ref[b, :, rank:] = lo
        hi, lo = split(khatri.T)
        flipped_ref[b, :, :n_rows] = hi
        flipped_ref[b, :, n_rows:] = lo
    for copy in loads:
        copy.wait()


def prepared(tensor, var, snap):
    nv, ns, width = tensor.shape
    rank = var.shape[1]
    blocks = 2
    return pl.pallas_call(
        prepare,
        name="prepare",
        in_specs=[hbm] * 3,
        out_specs=[vmem] * 5,
        out_shape=[
            jax.ShapeDtypeStruct((nv // blocks, ns, width), f32),
            jax.ShapeDtypeStruct((blocks, nv * ns // blocks, 2 * rank), bf16),
            jax.ShapeDtypeStruct((blocks, rank, 2 * nv * ns // blocks), bf16),
            jax.ShapeDtypeStruct(var.shape, f32),
            jax.ShapeDtypeStruct(snap.shape, f32),
        ],
        scratch_shapes=[pltpu.SemaphoreType.DMA(()), pltpu.SemaphoreType.DMA((2,))],
        compiler_params=small,
        cost_estimate=pl.CostEstimate(flops=0, bytes_accessed=8 * nv * ns * width, transcendentals=0),
    )(hold(tensor), hold(var), hold(snap))


def contract(tensor_hbm, data_ref, khatri_ref, flipped_ref, var_ref, snap_ref, mine_ref, other_ref,
             kept_ref, given_ref, snaps_ref, late_ref, across, down, total, sem):
    groups, own, rank = mine_ref.shape
    step, ns, width = data_ref.shape
    blocks, n_rows = khatri_ref.shape[:2]
    tiles, per = width // tile, tile // own // 2
    even = lax.axis_index("core") == 0

    def sides(a, b):
        return jnp.where(even, a, b), jnp.where(even, b, a)

    load = pltpu.make_async_copy(tensor_hbm.at[pl.ds(step, step)], late_ref, sem)
    load.start()
    snap_sum = jnp.zeros((ns, rank), f32)
    for b in range(blocks):
        if b == 1:
            load.wait()
        source = data_ref if b == 0 else late_ref
        k2, kt2 = khatri_ref[b], flipped_ref[b]
        k3 = jnp.concatenate([k2, k2[:, :rank]], axis=1)
        kt3 = jnp.concatenate([kt2, kt2[:, :n_rows]], axis=1)
        folded = jnp.zeros((n_rows, rank), f32)
        for n in range(tiles):
            if b == 0:
                block = [part for g in range(n * per, (n + 1) * per) for part in sides(mine_ref[g], other_ref[g])]
                block = jnp.concatenate(block, axis=0)
                hi, lo = split(block)
                down[n] = jnp.concatenate([hi, hi, lo], axis=0)
                hi, lo = split(block.T)
                across[n] = jnp.concatenate([hi, hi, lo], axis=0)
            model = dot(k3, across[n])
            data = source[:, :, n * tile:(n + 1) * tile].reshape(n_rows, tile)
            hi, lo = split((model - data) * lax.rsqrt(model))
            folded = folded + dot(jnp.concatenate([hi, lo, hi], axis=1), down[n])
            part = dot(kt3, jnp.concatenate([hi, hi, lo], axis=0))
            if b == 0:
                total[n] = part
            else:
                block = (total[n] + part).T
                for i in range(per):
                    first, second = block[2 * i * own:(2 * i + 1) * own], block[(2 * i + 1) * own:(2 * i + 2) * own]
                    kept_ref[n * per + i], given_ref[n * per + i] = sides(first, second)
        folded = folded.reshape(step, ns, rank)
        sums = (folded * snap_ref[...][None]).sum(1)
        kept_ref[groups, b * step:(b + 1) * step, :] = sums
        given_ref[groups, b * step:(b + 1) * step, :] = sums
        snap_sum = snap_sum + (folded * var_ref[b * step:(b + 1) * step, :][:, None, :]).sum(0)
    snaps_ref[...] = snap_sum


def contracted(tensor, ready, mine, other):
    groups, own, rank = mine.shape
    nv, ns, width = tensor.shape
    tiles = width // tile
    halfsum = jax.ShapeDtypeStruct((groups + 1, own, rank), f32)
    return pl.pallas_call(
        contract,
        name="contract",
        in_specs=[hbm] + [vmem] * 7,
        out_specs=[vmem] * 3,
        out_shape=[halfsum, halfsum, jax.ShapeDtypeStruct((ns, rank), f32)],
        scratch_shapes=[
            pltpu.VMEM((nv // 2, ns, width), f32),
            pltpu.VMEM((tiles, 3 * rank, tile), bf16),
            pltpu.VMEM((tiles, 3 * tile, rank), bf16),
            pltpu.VMEM((tiles, rank, tile), f32),
            pltpu.SemaphoreType.DMA(()),
        ],
        compiler_params=pltpu.CompilerParams(vmem_limit_bytes=24 << 20),
        cost_estimate=pl.CostEstimate(
            flops=18 * nv * ns * width * rank, bytes_accessed=4 * nv * ns * width, transcendentals=nv * ns * width
        ),
    )(hold(tensor), *ready, mine, other)


units = 19


def pack(kept_ref, got_ref, snaps_ref, out_ref):
    own, rank = kept_ref.shape[1:]
    ns = snaps_ref.shape[0]
    for h in range(rank // lanes):
        side = slice(h * lanes, (h + 1) * lanes)
        rest = jnp.concatenate([snaps_ref[own:, side], jnp.zeros((2 * own - ns, lanes), f32)], axis=0)
        for u in range(units):
            if u < 17:
                block = kept_ref[u, :, side] + got_ref[u, :, side]
            else:
                block = snaps_ref[:own, side] if u == 17 else rest
            out_ref[pl.ds(h * own * units + u, own, stride=units), :] = block


def regroup(got_ref, out_ref):
    n = got_ref.shape[0] // units
    unit = lambda u: got_ref[pl.ds(u, n, stride=units), :]
    cells = jnp.concatenate([unit(u).sum(0, keepdims=True) for u in range(16)], axis=0)
    grid = lambda u: unit(u).reshape(8, 8, lanes)
    rest = jnp.concatenate([grid(16).sum(0), grid(17).sum(1), grid(18).sum(1)], axis=0)
    for x in range(4):
        out_ref[x, :8, :] = cells[8 * (x // 2):8 * (x // 2) + 8]
        out_ref[x, 8:, :] = rest


def combine(got_ref, out_ref):
    high, low = lax.axis_index("xh") == 0, lax.axis_index("xl") == 0
    part = lambda x, i, k: got_ref[x, 8 * i:8 * (i + k), :]
    cells = part(0, 0, 1) + part(1, 0, 1) + part(2, 0, 1) + part(3, 0, 1)
    var = jnp.where(low, part(0, 1, 1) + part(2, 1, 1), part(1, 1, 1) + part(3, 1, 1))
    snap = jnp.where(high, part(0, 2, 2) + part(1, 2, 2), part(2, 2, 2) + part(3, 2, 2))
    shape = (8, 8, lanes)
    line = lax.broadcasted_iota(jnp.int32, shape, 1)
    each = lambda a: jnp.broadcast_to(a[:, None], shape)
    base = jnp.where(line % 4 == 0, each(cells), jnp.where(line % 4 == 2, each(snap[:8]), each(snap[8:])))
    var = each(var)
    for k in range(4):
        pair = jnp.where(line[0] < 4, var[2 * k], var[2 * k + 1])
        block = jnp.where(line % 4 == 1, pair[None], base)
        for y in range(8):
            out_ref[32 * y + 8 * k:32 * y + 8 * k + 8, :] = block[y]


def unpack(got_ref, cells_ref, var_ref, snap_ref):
    own = cells_ref.shape[0]
    ns = snap_ref.shape[0]
    for h in range(2):
        side = slice(h * lanes, (h + 1) * lanes)
        part = lambda u, k: got_ref[pl.ds(4 * h * own + u, k, stride=4), :]
        cells_ref[:, side] = part(0, own)
        var_ref[:, side] = part(1, own)
        snap_ref[:own, side] = part(2, own)
        snap_ref[own:, side] = part(3, ns - own)


plane = ("y", "z")


def exchange(a, n, axes):
    return lax.all_to_all(a.reshape(n, -1, 1, lanes), axes, 0, 0).reshape(-1, lanes)


def local(tensor, cell_factor, var_factor, snap_factor):
    groups, n = lax.axis_size(rows), lax.axis_size(plane)
    mine = lax.all_to_all(jnp.broadcast_to(cell_factor[None], (groups, *cell_factor.shape)), rows, 0, 0)
    other = lax.ppermute(mine, "core", swap)
    ready = prepared(tensor, var_factor, snap_factor)
    kept, given, part_snaps = contracted(tensor, ready, mine, other)
    got = lax.ppermute(given, "core", swap)

    def call(kernel, shapes, *args):
        return pl.pallas_call(
            kernel,
            name=kernel.__name__,
            in_specs=[vmem] * len(args),
            out_specs=[vmem] * len(shapes),
            out_shape=[jax.ShapeDtypeStruct(shape, f32) for shape in shapes],
            compiler_params=small,
        )(*args)

    (sent,) = call(pack, [(units * n, lanes)], kept, got, part_snaps)
    (sent,) = call(regroup, [(4, 32, lanes)], exchange(sent, n, plane))
    sent = lax.all_to_all(sent, ("xh", "xl"), 0, 0)
    (sent,) = call(combine, [(4 * n, lanes)], sent)
    return tuple(
        call(unpack, [a.shape for a in (cell_factor, var_factor, snap_factor)], exchange(sent, n, plane))
    )


def solution(mesh):
    fine = Mesh(mesh.devices.reshape(2, 8, 2, 8, 2), ("xh", "y", "core", "z", "xl"))
    return jax.shard_map(
        local,
        mesh=fine,
        in_specs=(P(variables, snaps, None), P(snaps, None), P(variables, None), P(snaps, None)),
        out_specs=(P(snaps, None), P(variables, None), P(snaps, None)),
        check_vma=False,
    )
```

```python
import functools

import jax
import jax.numpy as jnp
from jax import lax
from jax.experimental import pallas as pl
from jax.experimental.pallas import tpu as pltpu
from jax.sharding import Mesh, PartitionSpec as P


snaps = ("xh", "y", "core")
variables = ("z", "xl")
swap = [(0, 1), (1, 0)]
f32, bf16 = jnp.float32, jnp.bfloat16
lanes, tile = 128, 256
vmem = pl.BlockSpec(memory_space=pltpu.VMEM)
hbm = pl.BlockSpec(memory_space=pltpu.HBM)
small = pltpu.CompilerParams(vmem_limit_bytes=8 << 20)


def hold(a):
    return pltpu.with_memory_space_constraint(a, pltpu.HBM)


def split(a):
    hi = a.astype(bf16)
    return hi, (a - hi.astype(f32)).astype(bf16)


def dot(a, b):
    return jnp.dot(a, b, preferred_element_type=f32)


def prepare(tensor_hbm, var_hbm, snap_hbm, data_ref, khatri_ref, flipped_ref, var_ref, snap_ref, sem, small_sems):
    blocks, n_rows, rank = khatri_ref.shape[0], khatri_ref.shape[1], khatri_ref.shape[2] // 2
    step = data_ref.shape[0]
    factors = [
        pltpu.make_async_copy(snap_hbm, snap_ref, small_sems.at[0]),
        pltpu.make_async_copy(var_hbm, var_ref, small_sems.at[1]),
    ]
    loads = [pltpu.make_async_copy(tensor_hbm.at[pl.ds(0, step)], data_ref, sem)]
    for copy in factors + loads:
        copy.start()
    for copy in factors:
        copy.wait()
    for b in range(blocks):
        khatri = var_ref[b * step:(b + 1) * step, :][:, None, :] * snap_ref[...][None, :, :]
        khatri = khatri.reshape(n_rows, rank)
        hi, lo = split(khatri)
        khatri_ref[b, :, :rank] = hi
        khatri_ref[b, :, rank:] = lo
        hi, lo = split(khatri.T)
        flipped_ref[b, :, :n_rows] = hi
        flipped_ref[b, :, n_rows:] = lo
    for copy in loads:
        copy.wait()


def prepared(tensor, var, snap):
    nv, ns, width = tensor.shape
    rank = var.shape[1]
    blocks = 2
    return pl.pallas_call(
        prepare,
        name="prepare",
        in_specs=[hbm] * 3,
        out_specs=[vmem] * 5,
        out_shape=[
            jax.ShapeDtypeStruct((nv // blocks, ns, width), f32),
            jax.ShapeDtypeStruct((blocks, nv * ns // blocks, 2 * rank), bf16),
            jax.ShapeDtypeStruct((blocks, rank, 2 * nv * ns // blocks), bf16),
            jax.ShapeDtypeStruct(var.shape, f32),
            jax.ShapeDtypeStruct(snap.shape, f32),
        ],
        scratch_shapes=[pltpu.SemaphoreType.DMA(()), pltpu.SemaphoreType.DMA((2,))],
        compiler_params=small,
        cost_estimate=pl.CostEstimate(flops=0, bytes_accessed=8 * nv * ns * width, transcendentals=0),
    )(hold(tensor), hold(var), hold(snap))


def contract(stage, tensor_hbm, data_ref, khatri_ref, flipped_ref, var_ref, snap_ref, mine_ref, other_ref, *refs):
    own, rank = mine_ref.shape[1:]
    step, ns, width = data_ref.shape
    blocks, n_rows = khatri_ref.shape[:2]
    half = width // 2
    tiles, per = half // tile // (2 - stage // 2), tile // own // 2
    skip = per * tiles if stage == 1 else 0
    if stage > 0:
        before_ref, *refs = refs
    if stage == 2:
        early, refs = refs[:2], refs[2:]
    kept_ref, given_ref, last_ref, late_ref, across, down, total, sem = refs
    even, x = lax.axis_index("core") == 0, lax.axis_index("xh")
    start = (x if stage < 2 else 1 - x) * half + (tile if stage == 1 else 0)

    def sides(a, b):
        return jnp.where(even, a, b), jnp.where(even, b, a)

    columns = pl.ds(pl.multiple_of(start, tile), tiles * tile)
    load = pltpu.make_async_copy(tensor_hbm.at[pl.ds(step, step), :, columns], late_ref, sem)
    load.start()
    shift = 0
    if stage == 2:
        shift = 2 * early[0].shape[0]
        for i, ref in enumerate(early):
            given_ref[i * ref.shape[0]:(i + 1) * ref.shape[0]] = ref[...]
    snap_sum = jnp.zeros((ns, rank), f32)
    for b in range(blocks):
        if b == 1:
            load.wait()
        k2, kt2 = khatri_ref[b], flipped_ref[b]
        k3 = jnp.concatenate([k2, k2[:, :rank]], axis=1)
        kt3 = jnp.concatenate([kt2, kt2[:, :n_rows]], axis=1)
        folded = before_ref[b] if stage > 0 else jnp.zeros((n_rows, rank), f32)
        for n in range(tiles):
            if b == 0:
                near = range(skip + n * per, skip + (n + 1) * per)
                block = [part for g in near for part in sides(mine_ref[g], other_ref[g])]
                block = jnp.concatenate(block, axis=0)
                hi, lo = split(block)
                down[n] = jnp.concatenate([hi, hi, lo], axis=0)
                hi, lo = split(block.T)
                across[n] = jnp.concatenate([hi, hi, lo], axis=0)
            model = dot(k3, across[n])
            if b == 0:
                data = data_ref[:, :, pl.ds(pl.multiple_of(start + n * tile, tile), tile)]
            else:
                data = late_ref[:, :, n * tile:(n + 1) * tile]
            hi, lo = split((model - data.reshape(n_rows, tile)) * lax.rsqrt(model))
            folded = folded + dot(jnp.concatenate([hi, lo, hi], axis=1), down[n])
            part = dot(kt3, jnp.concatenate([hi, hi, lo], axis=0))
            if b == 0:
                total[n] = part
            else:
                block = (total[n] + part).T
                for i in range(per):
                    first, second = block[2 * i * own:(2 * i + 1) * own], block[(2 * i + 1) * own:(2 * i + 2) * own]
                    kept_ref[n * per + i], given_ref[shift + n * per + i] = sides(first, second)
        if stage < 2:
            last_ref[b] = folded
            continue
        folded = folded.reshape(step, ns, rank)
        sums = (folded * snap_ref[...][None]).sum(1)
        kept_ref[tiles * per, b * step:(b + 1) * step, :] = sums
        given_ref[shift + tiles * per, b * step:(b + 1) * step, :] = sums
        snap_sum = snap_sum + (folded * var_ref[b * step:(b + 1) * step, :][:, None, :]).sum(0)
    if stage == 2:
        last_ref[...] = snap_sum


def contracted(stage, tensor, ready, mine, other, *more):
    groups, own, rank = mine.shape
    nv, ns, width = tensor.shape
    tiles = width // 2 // tile // (2 - stage // 2)
    shape = lambda *a: jax.ShapeDtypeStruct(a, f32)
    if stage < 2:
        outs = [shape(groups // 2, own, rank), shape(groups // 2, own, rank), shape(2, nv * ns // 2, rank)]
    else:
        outs = [shape(groups + 1, own, rank), shape(2 * groups + 1, own, rank), shape(ns, rank)]
    work = nv * ns * tiles * tile
    return pl.pallas_call(
        functools.partial(contract, stage),
        name="contract",
        in_specs=[hbm] + [vmem] * (7 + len(more)),
        out_specs=[vmem] * 3,
        out_shape=outs,
        scratch_shapes=[
            pltpu.VMEM((nv // 2, ns, tiles * tile), f32),
            pltpu.VMEM((tiles, 3 * rank, tile), bf16),
            pltpu.VMEM((tiles, 3 * tile, rank), bf16),
            pltpu.VMEM((tiles, rank, tile), f32),
            pltpu.SemaphoreType.DMA(()),
        ],
        compiler_params=pltpu.CompilerParams(vmem_limit_bytes=24 << 20),
        cost_estimate=pl.CostEstimate(flops=18 * work * rank, bytes_accessed=4 * work, transcendentals=work),
    )(hold(tensor), *ready, mine, other, *more)


units = 19


def pack(first_ref, second_ref, third_ref, got_ref, snaps_ref, out_ref):
    own, rank = first_ref.shape[1:]
    kept = [(ref, i) for ref in (first_ref, second_ref, third_ref) for i in range(ref.shape[0])]
    ns = snaps_ref.shape[0]
    for h in range(rank // lanes):
        side = slice(h * lanes, (h + 1) * lanes)
        rest = jnp.concatenate([snaps_ref[own:, side], jnp.zeros((2 * own - ns, lanes), f32)], axis=0)
        for u in range(units):
            if u < 17:
                block = kept[u][0][kept[u][1], :, side] + got_ref[u, :, side]
            else:
                block = snaps_ref[:own, side] if u == 17 else rest
            out_ref[pl.ds(h * own * units + u, own, stride=units), :] = block


def regroup(got_ref, out_ref):
    n = got_ref.shape[0] // units
    unit = lambda u: got_ref[pl.ds(u, n, stride=units), :]
    cells = jnp.concatenate([unit(u).sum(0, keepdims=True) for u in range(16)], axis=0)
    grid = lambda u: unit(u).reshape(8, 8, lanes)
    rest = jnp.concatenate([grid(16).sum(0), grid(17).sum(1), grid(18).sum(1)], axis=0)
    for x in range(4):
        out_ref[x, :8, :] = jnp.where(lax.axis_index("xh") == x // 2, cells[:8], cells[8:])
        out_ref[x, 8:, :] = rest


def combine(got_ref, out_ref):
    high, low = lax.axis_index("xh") == 0, lax.axis_index("xl") == 0
    part = lambda x, i, k: got_ref[x, 8 * i:8 * (i + k), :]
    cells = part(0, 0, 1) + part(1, 0, 1) + part(2, 0, 1) + part(3, 0, 1)
    var = jnp.where(low, part(0, 1, 1) + part(2, 1, 1), part(1, 1, 1) + part(3, 1, 1))
    snap = jnp.where(high, part(0, 2, 2) + part(1, 2, 2), part(2, 2, 2) + part(3, 2, 2))
    shape = (8, 8, lanes)
    line = lax.broadcasted_iota(jnp.int32, shape, 1)
    each = lambda a: jnp.broadcast_to(a[:, None], shape)
    base = jnp.where(line % 4 == 0, each(cells), jnp.where(line % 4 == 2, each(snap[:8]), each(snap[8:])))
    var = each(var)
    for k in range(4):
        pair = jnp.where(line[0] < 4, var[2 * k], var[2 * k + 1])
        block = jnp.where(line % 4 == 1, pair[None], base)
        for y in range(8):
            out_ref[32 * y + 8 * k:32 * y + 8 * k + 8, :] = block[y]


def unpack(got_ref, cells_ref, var_ref, snap_ref):
    own = cells_ref.shape[0]
    ns = snap_ref.shape[0]
    for h in range(2):
        side = slice(h * lanes, (h + 1) * lanes)
        part = lambda u, k: got_ref[pl.ds(4 * h * own + u, k, stride=4), :]
        cells_ref[:, side] = part(0, own)
        var_ref[:, side] = part(1, own)
        snap_ref[:own, side] = part(2, own)
        snap_ref[own:, side] = part(3, ns - own)


plane = ("y", "z")


def exchange(a, n, axes):
    return lax.all_to_all(a.reshape(n, -1, 1, lanes), axes, 0, 0).reshape(-1, lanes)


def local(tensor, cell_factor, var_factor, snap_factor):
    near, n = lax.axis_size("y"), lax.axis_size(plane)
    mine = lax.all_to_all(jnp.broadcast_to(cell_factor[None], (near, *cell_factor.shape)), "y", 0, 0)
    far = lax.ppermute(mine, ("xh", "xl"), [(0, 3), (3, 0), (1, 2), (2, 1)])
    other = lax.ppermute(mine, "core", swap)
    ready = prepared(tensor, var_factor, snap_factor)
    kept0, given0, folded = contracted(0, tensor, ready, mine, other)
    far_other = lax.ppermute(far, "core", swap)
    kept1, given1, folded = contracted(1, tensor, ready, mine, other, folded)
    kept2, given, part_snaps = contracted(2, tensor, ready, far, far_other, folded, given0, given1)
    got = lax.ppermute(given, "core", swap)

    def call(kernel, shapes, *args):
        return pl.pallas_call(
            kernel,
            in_specs=[vmem] * len(args),
            out_specs=[vmem] * len(shapes),
            out_shape=[jax.ShapeDtypeStruct(shape, f32) for shape in shapes],
            compiler_params=small,
        )(*args)

    (sent,) = call(pack, [(units * n, lanes)], kept0, kept1, kept2, got, part_snaps)
    (sent,) = call(regroup, [(4, 32, lanes)], exchange(sent, n, plane))
    sent = lax.all_to_all(sent, ("xh", "xl"), 0, 0)
    (sent,) = call(combine, [(4 * n, lanes)], sent)
    return tuple(
        call(unpack, [a.shape for a in (cell_factor, var_factor, snap_factor)], exchange(sent, n, plane))
    )


def solution(mesh):
    fine = Mesh(mesh.devices.reshape(2, 8, 2, 8, 2), ("xh", "y", "core", "z", "xl"))
    return jax.shard_map(
        local,
        mesh=fine,
        in_specs=(P(variables, snaps, None), P(snaps, None), P(variables, None), P(snaps, None)),
        out_specs=(P(snaps, None), P(variables, None), P(snaps, None)),
        check_vma=False,
    )
```

```python
import functools

import jax
import jax.numpy as jnp
from jax import lax
from jax.experimental import pallas as pl
from jax.experimental.pallas import tpu as pltpu
from jax.sharding import Mesh, PartitionSpec as P


snaps = ("xh", "y", "core")
variables = ("z", "xl")
swap = [(0, 1), (1, 0)]
f32, bf16 = jnp.float32, jnp.bfloat16
lanes, tile = 128, 256
vmem = pl.BlockSpec(memory_space=pltpu.VMEM)
hbm = pl.BlockSpec(memory_space=pltpu.HBM)
small = pltpu.CompilerParams(vmem_limit_bytes=8 << 20)


def hold(a):
    return pltpu.with_memory_space_constraint(a, pltpu.HBM)


def split(a):
    hi = a.astype(bf16)
    return hi, (a - hi.astype(f32)).astype(bf16)


def dot(a, b):
    return jnp.dot(a, b, preferred_element_type=f32)


def prepare(tensor_hbm, var_hbm, snap_hbm, data_ref, khatri_ref, flipped_ref, var_ref, snap_ref, sem, small_sems):
    blocks, n_rows, rank = khatri_ref.shape[0], khatri_ref.shape[1], khatri_ref.shape[2] // 2
    step = data_ref.shape[0]
    factors = [
        pltpu.make_async_copy(snap_hbm, snap_ref, small_sems.at[0]),
        pltpu.make_async_copy(var_hbm, var_ref, small_sems.at[1]),
    ]
    loads = [pltpu.make_async_copy(tensor_hbm.at[pl.ds(0, step)], data_ref, sem)]
    for copy in factors + loads:
        copy.start()
    for copy in factors:
        copy.wait()
    for b in range(blocks):
        khatri = var_ref[b * step:(b + 1) * step, :][:, None, :] * snap_ref[...][None, :, :]
        khatri = khatri.reshape(n_rows, rank)
        hi, lo = split(khatri)
        khatri_ref[b, :, :rank] = hi
        khatri_ref[b, :, rank:] = lo
        hi, lo = split(khatri.T)
        flipped_ref[b, :, :n_rows] = hi
        flipped_ref[b, :, n_rows:] = lo
    for copy in loads:
        copy.wait()


def prepared(tensor, var, snap):
    nv, ns, width = tensor.shape
    rank = var.shape[1]
    blocks = 2
    return pl.pallas_call(
        prepare,
        name="prepare",
        in_specs=[hbm] * 3,
        out_specs=[vmem] * 5,
        out_shape=[
            jax.ShapeDtypeStruct((nv // blocks, ns, width), f32),
            jax.ShapeDtypeStruct((blocks, nv * ns // blocks, 2 * rank), bf16),
            jax.ShapeDtypeStruct((blocks, rank, 2 * nv * ns // blocks), bf16),
            jax.ShapeDtypeStruct(var.shape, f32),
            jax.ShapeDtypeStruct(snap.shape, f32),
        ],
        scratch_shapes=[pltpu.SemaphoreType.DMA(()), pltpu.SemaphoreType.DMA((2,))],
        compiler_params=small,
        cost_estimate=pl.CostEstimate(flops=0, bytes_accessed=8 * nv * ns * width, transcendentals=0),
    )(hold(tensor), hold(var), hold(snap))


def contract(stage, tensor_hbm, data_ref, khatri_ref, flipped_ref, var_ref, snap_ref, mine_ref, other_ref, *refs):
    own, rank = mine_ref.shape[1:]
    step, ns, width = data_ref.shape
    blocks, n_rows = khatri_ref.shape[:2]
    half = width // 2
    tiles, per = half // tile // (2 - stage // 2), tile // own // 2
    skip = per * tiles if stage == 1 else 0
    if stage > 0:
        before_ref, *refs = refs
    if stage == 2:
        early, refs = refs[:2], refs[2:]
    kept_ref, given_ref, last_ref, late_ref, across, down, total, sem = refs
    even, x = lax.axis_index("core") == 0, lax.axis_index("xh")
    start = (x if stage < 2 else 1 - x) * half + (tile if stage == 1 else 0)

    def sides(a, b):
        return jnp.where(even, a, b), jnp.where(even, b, a)

    columns = pl.ds(pl.multiple_of(start, tile), tiles * tile)
    load = pltpu.make_async_copy(tensor_hbm.at[pl.ds(step, step), :, columns], late_ref, sem)
    load.start()
    shift = 0
    if stage == 2:
        shift = 2 * early[0].shape[0]
        for i, ref in enumerate(early):
            given_ref[i * ref.shape[0]:(i + 1) * ref.shape[0]] = ref[...]
    snap_sum = jnp.zeros((ns, rank), f32)
    for b in range(blocks):
        if b == 1:
            load.wait()
        k2, kt2 = khatri_ref[b], flipped_ref[b]
        k3 = jnp.concatenate([k2, k2[:, :rank]], axis=1)
        kt3 = jnp.concatenate([kt2, kt2[:, :n_rows]], axis=1)
        folded = before_ref[b] if stage > 0 else jnp.zeros((n_rows, rank), f32)
        for n in range(tiles):
            if b == 0:
                near = range(skip + n * per, skip + (n + 1) * per)
                block = [part for g in near for part in sides(mine_ref[g], other_ref[g])]
                block = jnp.concatenate(block, axis=0)
                hi, lo = split(block)
                down[n] = jnp.concatenate([hi, hi, lo], axis=0)
                if stage == 2:
                    across[n] = jnp.concatenate([hi, hi, lo], axis=1)
                else:
                    hi, lo = split(block.T)
                    across[n] = jnp.concatenate([hi, hi, lo], axis=0)
            if stage == 2:
                model = lax.dot_general(k3, across[n], (((1,), (1,)), ((), ())), preferred_element_type=f32)
            else:
                model = dot(k3, across[n])
            if b == 0:
                data = data_ref[:, :, pl.ds(pl.multiple_of(start + n * tile, tile), tile)]
            else:
                data = late_ref[:, :, n * tile:(n + 1) * tile]
            hi, lo = split((model - data.reshape(n_rows, tile)) * lax.rsqrt(model))
            folded = folded + dot(jnp.concatenate([hi, lo, hi], axis=1), down[n])
            part = dot(kt3, jnp.concatenate([hi, hi, lo], axis=0))
            if b == 0:
                total[n] = part
            else:
                block = (total[n] + part).T
                for i in range(per):
                    first, second = block[2 * i * own:(2 * i + 1) * own], block[(2 * i + 1) * own:(2 * i + 2) * own]
                    kept_ref[n * per + i], given_ref[shift + n * per + i] = sides(first, second)
        if stage < 2:
            last_ref[b] = folded
            continue
        folded = folded.reshape(step, ns, rank)
        sums = (folded * snap_ref[...][None]).sum(1)
        kept_ref[tiles * per, b * step:(b + 1) * step, :] = sums
        given_ref[shift + tiles * per, b * step:(b + 1) * step, :] = sums
        snap_sum = snap_sum + (folded * var_ref[b * step:(b + 1) * step, :][:, None, :]).sum(0)
    if stage == 2:
        last_ref[...] = snap_sum


def contracted(stage, tensor, ready, mine, other, *more):
    groups, own, rank = mine.shape
    nv, ns, width = tensor.shape
    tiles = width // 2 // tile // (2 - stage // 2)
    shape = lambda *a: jax.ShapeDtypeStruct(a, f32)
    if stage < 2:
        outs = [shape(groups // 2, own, rank), shape(groups // 2, own, rank), shape(2, nv * ns // 2, rank)]
    else:
        outs = [shape(groups + 1, own, rank), shape(2 * groups + 1, own, rank), shape(ns, rank)]
    work = nv * ns * tiles * tile
    return pl.pallas_call(
        functools.partial(contract, stage),
        name="contract",
        in_specs=[hbm] + [vmem] * (7 + len(more)),
        out_specs=[vmem] * 3,
        out_shape=outs,
        scratch_shapes=[
            pltpu.VMEM((nv // 2, ns, tiles * tile), f32),
            pltpu.VMEM((tiles, tile, 3 * rank) if stage == 2 else (tiles, 3 * rank, tile), bf16),
            pltpu.VMEM((tiles, 3 * tile, rank), bf16),
            pltpu.VMEM((tiles, rank, tile), f32),
            pltpu.SemaphoreType.DMA(()),
        ],
        compiler_params=pltpu.CompilerParams(vmem_limit_bytes=24 << 20),
        cost_estimate=pl.CostEstimate(flops=18 * work * rank, bytes_accessed=4 * work, transcendentals=work),
    )(hold(tensor), *ready, mine, other, *more)


units = 19


def pack(first_ref, second_ref, third_ref, got_ref, snaps_ref, out_ref):
    own, rank = first_ref.shape[1:]
    kept = [(ref, i) for ref in (first_ref, second_ref, third_ref) for i in range(ref.shape[0])]
    ns = snaps_ref.shape[0]
    for h in range(rank // lanes):
        side = slice(h * lanes, (h + 1) * lanes)
        rest = jnp.concatenate([snaps_ref[own:, side], jnp.zeros((2 * own - ns, lanes), f32)], axis=0)
        for u in range(units):
            if u < 17:
                block = kept[u][0][kept[u][1], :, side] + got_ref[u, :, side]
            else:
                block = snaps_ref[:own, side] if u == 17 else rest
            out_ref[pl.ds(h * own * units + u, own, stride=units), :] = block


def regroup(got_ref, out_ref):
    n = got_ref.shape[0] // units
    unit = lambda u: got_ref[pl.ds(u, n, stride=units), :]
    cells = jnp.concatenate([unit(u).sum(0, keepdims=True) for u in range(16)], axis=0)
    grid = lambda u: unit(u).reshape(8, 8, lanes)
    rest = jnp.concatenate([grid(16).sum(0), grid(17).sum(1), grid(18).sum(1)], axis=0)
    for x in range(4):
        out_ref[x, :8, :] = jnp.where(lax.axis_index("xh") == x // 2, cells[:8], cells[8:])
        out_ref[x, 8:, :] = rest


def combine(got_ref, out_ref):
    high, low = lax.axis_index("xh") == 0, lax.axis_index("xl") == 0
    part = lambda x, i, k: got_ref[x, 8 * i:8 * (i + k), :]
    cells = part(0, 0, 1) + part(1, 0, 1) + part(2, 0, 1) + part(3, 0, 1)
    var = jnp.where(low, part(0, 1, 1) + part(2, 1, 1), part(1, 1, 1) + part(3, 1, 1))
    snap = jnp.where(high, part(0, 2, 2) + part(1, 2, 2), part(2, 2, 2) + part(3, 2, 2))
    shape = (8, 8, lanes)
    line = lax.broadcasted_iota(jnp.int32, shape, 1)
    each = lambda a: jnp.broadcast_to(a[:, None], shape)
    base = jnp.where(line % 4 == 0, each(cells), jnp.where(line % 4 == 2, each(snap[:8]), each(snap[8:])))
    var = each(var)
    for k in range(4):
        pair = jnp.where(line[0] < 4, var[2 * k], var[2 * k + 1])
        block = jnp.where(line % 4 == 1, pair[None], base)
        for y in range(8):
            out_ref[32 * y + 8 * k:32 * y + 8 * k + 8, :] = block[y]


def unpack(got_ref, cells_ref, var_ref, snap_ref):
    own = cells_ref.shape[0]
    ns = snap_ref.shape[0]
    for h in range(2):
        side = slice(h * lanes, (h + 1) * lanes)
        part = lambda u, k: got_ref[pl.ds(4 * h * own + u, k, stride=4), :]
        cells_ref[:, side] = part(0, own)
        var_ref[:, side] = part(1, own)
        snap_ref[:own, side] = part(2, own)
        snap_ref[own:, side] = part(3, ns - own)


plane = ("y", "z")


def exchange(a, n, axes):
    return lax.all_to_all(a.reshape(n, -1, 1, lanes), axes, 0, 0).reshape(-1, lanes)


def local(tensor, cell_factor, var_factor, snap_factor):
    near, n = lax.axis_size("y"), lax.axis_size(plane)
    mine = lax.all_to_all(jnp.broadcast_to(cell_factor[None], (near, *cell_factor.shape)), "y", 0, 0)
    far = lax.ppermute(mine, ("xh", "xl"), [(0, 3), (3, 0), (1, 2), (2, 1)])
    other = lax.ppermute(mine, "core", swap)
    ready = prepared(tensor, var_factor, snap_factor)
    kept0, given0, folded = contracted(0, tensor, ready, mine, other)
    far_other = lax.ppermute(far, "core", swap)
    kept1, given1, folded = contracted(1, tensor, ready, mine, other, folded)
    kept2, given, part_snaps = contracted(2, tensor, ready, far, far_other, folded, given0, given1)
    got = lax.ppermute(given, "core", swap)

    def call(kernel, shapes, *args):
        return pl.pallas_call(
            kernel,
            in_specs=[vmem] * len(args),
            out_specs=[vmem] * len(shapes),
            out_shape=[jax.ShapeDtypeStruct(shape, f32) for shape in shapes],
            compiler_params=small,
        )(*args)

    (sent,) = call(pack, [(units * n, lanes)], kept0, kept1, kept2, got, part_snaps)
    (sent,) = call(regroup, [(4, 32, lanes)], exchange(sent, n, plane))
    sent = lax.all_to_all(sent, ("xh", "xl"), 0, 0)
    (sent,) = call(combine, [(4 * n, lanes)], sent)
    return tuple(
        call(unpack, [a.shape for a in (cell_factor, var_factor, snap_factor)], exchange(sent, n, plane))
    )


def solution(mesh):
    fine = Mesh(mesh.devices.reshape(2, 8, 2, 8, 2), ("xh", "y", "core", "z", "xl"))
    return jax.shard_map(
        local,
        mesh=fine,
        in_specs=(P(variables, snaps, None), P(snaps, None), P(variables, None), P(snaps, None)),
        out_specs=(P(snaps, None), P(variables, None), P(snaps, None)),
        check_vma=False,
    )
```
